32 devices in a mesh: pp: 2 (over core), cp: 4 (over y, x), tp: 4 (over z).
Axes of the slice: x: 2, y: 2, z: 4, core: 2. Of those that a mesh axis runs over, the one named last changes fastest.
Arguments:
- query: bfloat16 [2, 512, 4096], P('pp', 'cp', 'tp'), may hold values from -120 to 120
- keyval: bfloat16 [2, 2, 512, 1024], P('pp', None, 'cp', 'tp'), may hold values from -4 to 4
- out_weight: bfloat16 [2, 4096, 4096], P('pp', None, 'tp'), may hold values from -0.375 to 0.375
- residual: bfloat16 [2, 512, 4096], P('pp', 'cp', 'tp'), may hold values from -3 to 3
- block_order: int32 [8], replicated, may hold values from 0 to 7, as said below
Outputs:
- handed: bfloat16 [2, 512, 4096], P('pp', 'cp', 'tp')
The draws below stay inside these ranges and needn't reach their ends.
Inputs may be any that keep to these rules, and one draw needn't show every extreme that they name: A permutation of the 8 sequence blocks; context index c holds blocks block_order[2 c] and block_order[2 c + 1] in its first and second 64 rows.
All inputs are finite; a program needn't handle non-finite values.
Results may differ from the reference program's by a relative error of at most 0.013.
Values may be sent and summed in bfloat16 or wider, within the bound.
No kernel may reach another device: no remote copies, remote signals or barrier semaphores. Data moves between devices by JAX's collectives and lax.ppermute only.
A program may use at most 64 MiB of HBM per device.

```python
import math
import jax
import jax.numpy as jnp
from jax import lax

Q_DEV = 128
D = 4096
HD = 128
QHEADS = 32
KVHEADS = 8
GROUP = 4
HALF = 64
TOKENS = 512
BLOCKS = 8
SECTIONS = 2


def joint_draw(key):
    base_key = jax.random.fold_in(key, 7001)
    key_keys, key_vals, key_query = jax.random.split(base_key, 3)
    key_rows = jnp.clip(jax.random.normal(key_keys, (SECTIONS, TOKENS, KVHEADS, HD), jnp.float32), -4.0, 4.0)
    values = jnp.clip(jax.random.normal(key_vals, (SECTIONS, TOKENS, KVHEADS, HD), jnp.float32), -4.0, 4.0)
    queries = jnp.clip(jax.random.normal(key_query, (SECTIONS, TOKENS, QHEADS, HD), jnp.float32), -4.0, 4.0)
    return (queries, key_rows, values)


def draw_query(key, part):
    queries, key_rows, values = joint_draw(key)
    return queries.reshape(SECTIONS, TOKENS, QHEADS * HD).astype(jnp.bfloat16)


def draw_keyval(key, part):
    queries, key_rows, values = joint_draw(key)
    stacked = jnp.stack([key_rows, values], axis=1)
    return stacked.reshape(SECTIONS, 2, TOKENS, KVHEADS * HD).astype(jnp.bfloat16)


def draw_block_order(key, part):
    return jax.random.permutation(jax.random.fold_in(key, 9001), BLOCKS).astype(jnp.int32)


def block_scale(own_key, shape, shards, least, largest):
    gain, own = 1.0, jax.random.fold_in(own_key, 6)
    for axis_at, blocks in shards:
        heights = jnp.exp(jax.random.uniform(jax.random.fold_in(own, axis_at), (blocks,), jnp.float32, least / len(shards), largest / len(shards)))
        gain = gain * jnp.repeat(heights, shape[axis_at] // blocks).reshape([-1 if axis == axis_at else 1 for axis in range(len(shape))])
    return gain


def normal_values(key, extent, deviation, limit, shards=(), kind=jnp.bfloat16):
    gain = block_scale(key, extent, shards, -0.22, 0.18) if shards else 1.0
    values = jax.random.normal(key, extent, jnp.float32) * deviation * gain
    return jnp.minimum(jnp.maximum(values, -limit), limit).astype(kind)


def setup_inputs(seed: int = 0) -> dict:
    seeds = jax.random.split(jax.random.key(seed), 6)
    return {
        "query": draw_query(jax.random.fold_in(seeds[5], 71), 0),
        "keyval": draw_keyval(jax.random.fold_in(seeds[5], 71), 0),
        "out_weight": normal_values(seeds[2], (SECTIONS, QHEADS * HD, D), (QHEADS * HD // 16) ** -0.5, 0.375, ((0, 2), (2, 4))),
        "residual": normal_values(seeds[3], (SECTIONS, TOKENS, D), 0.5, 3.0, ((0, 2), (1, 4), (2, 4))),
        "block_order": draw_block_order(jax.random.fold_in(seeds[5], 71), 0),
    }


def token_positions(block_order):
    row_index = jnp.arange(TOKENS, dtype=jnp.int32)
    offsets = row_index % Q_DEV
    slot_index = (2 * (row_index // Q_DEV) + offsets // HALF).astype(jnp.int32)
    return block_order[slot_index] * HALF + offsets % HALF

def reference(query, keyval, out_weight, residual, block_order):
    places = token_positions(block_order)
    visible = places[None, :] <= places[:, None]
    results = []
    for section_index in range(SECTIONS):
        per_head = []
        for head_index in range(QHEADS):
            group_index = head_index // GROUP
            key_rows = keyval[section_index, 0, :, group_index * HD:(group_index + 1) * HD]
            values = keyval[section_index, 1, :, group_index * HD:(group_index + 1) * HD]
            head_query = query[section_index, :, head_index * HD:(head_index + 1) * HD]
            scores = jnp.dot(head_query, key_rows.T, preferred_element_type=jnp.float32) * (1.0 / math.sqrt(HD))
            scores = jnp.where(visible, scores, -1e+30)
            row_peak = lax.optimization_barrier(jnp.max(scores, axis=1, keepdims=True))
            weights = jnp.where(visible, jnp.exp(scores - row_peak), 0.0)
            row_mass = lax.optimization_barrier(jnp.sum(weights, axis=1, keepdims=True))
            rounded = weights.astype(jnp.bfloat16)
            summed = jnp.dot(rounded, values, preferred_element_type=jnp.float32)
            per_head.append((summed / row_mass).astype(jnp.bfloat16))
        attended = jnp.concatenate(per_head, axis=1)
        mixed_sum = jnp.dot(attended, out_weight[section_index], preferred_element_type=jnp.float32)
        mixed_sum = mixed_sum + residual[section_index].astype(jnp.float32)
        results.append(mixed_sum.astype(jnp.bfloat16))
    layer_out = jnp.stack(results)
    return jnp.roll(layer_out, 1, axis=0)
```

```python
import functools
import math

import jax
import jax.numpy as jnp
from jax import lax
from jax.experimental import pallas as pl
from jax.experimental.pallas import tpu as pltpu
from jax.sharding import PartitionSpec as P

HD = 128
GROUP = 4

LOW_SCORE = -1e30


def shifted(value, axis, steps):
    count = lax.axis_size(axis)
    pairs = [(source, (source + steps) % count) for source in range(count)]
    return lax.ppermute(value, axis, pairs)


def positions(row_index, block_order, shard_rows, half_rows):
    slot_index = 2 * (row_index // shard_rows) + row_index % shard_rows // half_rows
    lookup = jnp.arange(block_order.shape[0], dtype=jnp.int32)
    picked = jnp.sum(
        jnp.where(slot_index[:, None] == lookup[None, :], block_order[None, :], 0), axis=1
    )
    return picked * half_rows + row_index % half_rows


def attend_piece(carried, queries, query_pos, key_rows, values, key_pos):
    weighted, row_peak, row_mass = carried
    scores = jnp.einsum("qkgd,nkd->qkgn", queries, key_rows, preferred_element_type=jnp.float32) * (
        1.0 / math.sqrt(HD)
    )
    visible = (key_pos[None, :] <= query_pos[:, None])[:, None, None, :]
    scores = jnp.where(visible, scores, LOW_SCORE)
    new_peak = jnp.maximum(row_peak, jnp.max(scores, axis=3))
    factor = jnp.exp(row_peak - new_peak)
    weights = jnp.where(visible, jnp.exp(scores - new_peak[..., None]), 0.0)
    rounded = weights.astype(jnp.bfloat16)
    weighted = weighted * factor[..., None] + jnp.einsum(
        "qkgn,nkd->qkgd", rounded, values, preferred_element_type=jnp.float32
    )
    row_mass = row_mass * factor + jnp.sum(weights, axis=3)
    return (weighted, new_peak, row_mass)


def fold_rows(carried, queries, query_pos, key_rows, values, key_pos):
    total = key_rows.shape[0]
    if total <= 512 or total % 512 != 0:
        return attend_piece(carried, queries, query_pos, key_rows, values, key_pos)
    count = total // 512
    stacked = (
        key_rows.reshape((count, 512) + key_rows.shape[1:]),
        values.reshape((count, 512) + values.shape[1:]),
        key_pos.reshape(count, 512),
    )

    def advance(inner, block_in):
        return (attend_piece(inner, queries, query_pos, block_in[0], block_in[1], block_in[2]), None)

    result, unused = lax.scan(advance, carried, stacked)
    return result


def attend_plain(query, keyval, block_order):
    shard_rows = query.shape[1]
    half_rows = shard_rows // 2
    cp_index = lax.axis_index("cp")
    own_rows = cp_index * shard_rows + jnp.arange(shard_rows, dtype=jnp.int32)
    query_pos = positions(own_rows, block_order, shard_rows, half_rows)
    kv_count = keyval.shape[3] // HD
    queries = query[0].reshape(shard_rows, kv_count, GROUP, HD)
    block_in = lax.all_gather(keyval, "cp", axis=2, tiled=True)
    piece_rows = block_in.shape[2]
    row_index = jnp.arange(piece_rows, dtype=jnp.int32)
    key_pos = positions(row_index, block_order, shard_rows, half_rows)
    key_rows = block_in[0, 0].reshape(piece_rows, kv_count, HD)
    values = block_in[0, 1].reshape(piece_rows, kv_count, HD)
    start = (
        jnp.zeros((shard_rows, kv_count, GROUP, HD), jnp.float32),
        jnp.full((shard_rows, kv_count, GROUP), LOW_SCORE, jnp.float32),
        jnp.zeros((shard_rows, kv_count, GROUP), jnp.float32),
    )
    weighted, row_peak, row_mass = fold_rows(
        start, queries, query_pos, key_rows, values, key_pos
    )
    own = (weighted / row_mass[..., None]).astype(jnp.bfloat16)
    return [own[:, kv].reshape(shard_rows, GROUP * HD) for kv in range(kv_count)]


def attend_kernel(count, bias_ref, q_ref, *refs):
    kv_refs, out_ref = refs[:count], refs[count]
    bias = bias_ref[...]
    keys = jnp.concatenate([kv[0, 0] for kv in kv_refs], axis=0)
    values = jnp.concatenate([kv[0, 1] for kv in kv_refs], axis=0)
    for head in range(GROUP):
        lanes = pl.ds(head * HD, HD)
        scores = lax.dot_general(
            q_ref[0, :, lanes], keys, (((1,), (1,)), ((), ())), preferred_element_type=jnp.float32
        ) * (1.0 / math.sqrt(HD))
        scores = scores + bias
        weights = jnp.exp(scores - jnp.max(scores, axis=1, keepdims=True))
        mass = jnp.sum(weights, axis=1, keepdims=True)
        summed = jnp.dot(
            weights.astype(jnp.bfloat16), values, preferred_element_type=jnp.float32
        )
        out_ref[:, lanes] = (summed / mass).astype(out_ref.dtype)


def attend_group(group, bias, query, pieces):
    rows = query.shape[1]
    width = GROUP * HD
    keys = sum(piece.shape[2] for piece in pieces)
    return pl.pallas_call(
        functools.partial(attend_kernel, len(pieces)),
        grid=(1,),
        out_shape=jax.ShapeDtypeStruct((rows, width), jnp.bfloat16),
        in_specs=[
            pl.BlockSpec(bias.shape, lambda i: (0, 0)),
            pl.BlockSpec((1, rows, width), lambda i: (0, 0, group)),
        ]
        + [
            pl.BlockSpec((1, 2, piece.shape[2], HD), lambda i: (0, 0, 0, group))
            for piece in pieces
        ],
        out_specs=pl.BlockSpec((rows, width), lambda i: (0, 0)),
        compiler_params=pltpu.CompilerParams(vmem_limit_bytes=16 << 20),
        cost_estimate=pl.CostEstimate(
            flops=4 * rows * keys * width,
            bytes_accessed=4 * rows * width + 4 * rows * keys + 4 * keys * HD,
            transcendentals=rows * keys * GROUP,
        ),
    )(bias, query, *pieces)


def project_kernel(count, first, last, index_ref, *refs):
    refs = list(refs)
    lhs = [refs.pop(0) for _ in range(count)]
    rhs = [refs.pop(0) for _ in range(count)]
    total = None if first else refs.pop(0)[...]
    if last:
        total = total + refs.pop(0)[0].astype(jnp.float32)
    for a, b in zip(lhs, rhs):
        part = jnp.dot(a[...], b[0], preferred_element_type=jnp.float32)
        total = part if total is None else total + part
    out_ref = refs.pop(0)
    if last:
        out_ref[0] = total.astype(out_ref.dtype)
    else:
        out_ref[...] = total


def project(pieces, index, weight, total, residual):
    rows, depth = pieces[0].shape
    columns = weight.shape[2]
    wide = 512 if columns % 512 == 0 else columns
    count = len(pieces)

    def block_of(j):
        return lambda i, at: (0, at[j], i)

    operands = list(pieces) + [weight] * count
    specs = [pl.BlockSpec((rows, depth), lambda i, at: (0, 0))] * count
    specs += [pl.BlockSpec((1, depth, wide), block_of(j)) for j in range(count)]
    if total is not None:
        operands.append(total)
        specs.append(pl.BlockSpec((rows, wide), lambda i, at: (0, i)))
    if residual is not None:
        operands.append(residual)
        specs.append(pl.BlockSpec((1, rows, wide), lambda i, at: (0, 0, i)))
        shape = jax.ShapeDtypeStruct((1, rows, columns), jnp.bfloat16)
        out_spec = pl.BlockSpec((1, rows, wide), lambda i, at: (0, 0, i))
    else:
        shape = jax.ShapeDtypeStruct((rows, columns), jnp.float32)
        out_spec = pl.BlockSpec((rows, wide), lambda i, at: (0, i))
    return pl.pallas_call(
        functools.partial(project_kernel, count, total is None, residual is not None),
        out_shape=shape,
        grid_spec=pltpu.PrefetchScalarGridSpec(
            num_scalar_prefetch=1,
            grid=(columns // wide,),
            in_specs=specs,
            out_specs=out_spec,
        ),
        compiler_params=pltpu.CompilerParams(vmem_limit_bytes=24 << 20),
        cost_estimate=pl.CostEstimate(
            flops=2 * count * rows * depth * columns,
            bytes_accessed=2 * count * depth * (columns + rows) + 8 * rows * columns,
            transcendentals=0,
        ),
    )(index, *operands)


def folded_ring(count):
    return [0] + list(range(1, count, 2)) + list(range((count - 1) // 2 * 2, 0, -2))


def pick(table, at):
    table = jnp.asarray(table, jnp.int32)
    return jnp.sum(jnp.where(jnp.arange(table.shape[0]) == at, table, 0))


def attend_small(query, keyval, block_order):
    count = lax.axis_size("cp")
    shard_rows = query.shape[1]
    half_rows = shard_rows // 2
    cp_index = lax.axis_index("cp")
    pieces = [keyval] + [
        lax.ppermute(keyval, "cp", [(source, source ^ step) for source in range(count)])
        for step in range(1, count)
    ]
    own_rows = cp_index * shard_rows + jnp.arange(shard_rows, dtype=jnp.int32)
    query_pos = positions(own_rows, block_order, shard_rows, half_rows)
    row_index = jnp.arange(count * shard_rows, dtype=jnp.int32)
    row_index = (row_index // shard_rows ^ cp_index) * shard_rows + row_index % shard_rows
    key_pos = positions(row_index, block_order, shard_rows, half_rows)
    bias = jnp.where(key_pos[None, :] <= query_pos[:, None], 0.0, LOW_SCORE).astype(jnp.float32)
    kv_count = keyval.shape[3] // HD
    return [attend_group(group, bias, query, pieces) for group in range(kv_count)]


def local(query, keyval, out_weight, residual, block_order):
    cp_count = lax.axis_size("cp")
    tp_count = lax.axis_size("tp")
    shard_rows = query.shape[1]
    small = cp_count * shard_rows <= 1024 and cp_count & (cp_count - 1) == 0
    groups = (attend_small if small else attend_plain)(query, keyval, block_order)
    if tp_count == 4 and len(groups) == 2:
        ring = folded_ring(tp_count)
        forth = [(ring[at], ring[(at + 1) % tp_count]) for at in range(tp_count)]
        back = [(b, a) for a, b in forth]
        me = lax.axis_index("tp")
        came_forth = pick([a for a, b in sorted(forth, key=lambda p: p[1])], me)
        came_back = pick([a for a, b in sorted(back, key=lambda p: p[1])], me)
        across = 6 - me - came_forth - came_back
        low, high = groups
        low_forth = lax.ppermute(low, "tp", forth)
        low_back = lax.ppermute(low, "tp", back)
        high_back = lax.ppermute(high, "tp", back)
        high_forth = lax.ppermute(high, "tp", forth)
        low_across = lax.ppermute(low_forth, "tp", forth)
        high_across = lax.ppermute(high_back, "tp", back)
        at = lambda *places: jnp.stack(places)
        total = project([low, high], at(2 * me, 2 * me + 1), out_weight, None, None)
        total = project(
            [low_forth, low_back], at(2 * came_forth, 2 * came_back), out_weight, total, None
        )
        total = project(
            [high_back, high_forth, low_across],
            at(2 * came_back + 1, 2 * came_forth + 1, 2 * across),
            out_weight,
            total,
            None,
        )
        layer_out = project(
            [high_across], at(2 * across + 1), out_weight, total, residual
        )
    else:
        attended = lax.all_gather(jnp.concatenate(groups, axis=1), "tp", axis=1, tiled=True)
        mixed_sum = jnp.dot(attended, out_weight[0], preferred_element_type=jnp.float32)
        layer_out = (mixed_sum + residual[0].astype(jnp.float32)).astype(jnp.bfloat16)[None]
    return shifted(layer_out, "pp", 1)


def solution(mesh):
    placed = (
        P("pp", "cp", "tp"),
        P("pp", None, "cp", "tp"),
        P("pp", None, "tp"),
        P("pp", "cp", "tp"),
        P(),
    )
    return jax.shard_map(
        local, mesh=mesh, in_specs=placed, out_specs=P("pp", "cp", "tp"), check_vma=False
    )
```
